128 devices in a mesh: tgt: 8 (over x, y_lo), hist: 16 (over y_hi, z, core).
Axes of the slice: x: 4, y: 4 (y_hi: 2, y_lo: 2; y = y_hi * 2 + y_lo), z: 4, core: 2. Of those that a mesh axis runs over, the one named last changes fastest.
Arguments:
- history: float32 [2, 64, 64, 128, 128], P(None, 'hist', 'tgt'), may hold values from -6 to 6
- self_energy: float32 [2, 64, 128, 128], P(None, 'hist'), may hold values from -6 to 6
- green_row: float32 [2, 64, 128, 128], P(None, 'tgt'), may hold values from -6 to 6
- propagator: float32 [2, 128, 128], replicated, may hold values from -0.375 to 0.375
Outputs:
- new_rows: float32 [4, 2, 64, 128, 128], P(None, None, 'tgt', 'hist')
The draws below stay inside these ranges and needn't reach their ends.
All inputs are finite; a program needn't handle non-finite values.
Results may differ from the reference program's by a relative error of at most 0.00016.
Values sent between devices are 32-bit elements; how exact they have to be, the bound alone decides.
No kernel may reach another device: no remote copies, remote signals or barrier semaphores. Data moves between devices by JAX's collectives and lax.ppermute only.
A program may use at most 64 MiB of HBM per device.

```python
import jax
import jax.numpy as jnp
from jax import lax

N = 128
SH = 4
STEPS = 4
TW = 64
TT = 8


def block_levels(stream_key, shape, shards, smallest, top_value):
    loudness, own = 1.0, jax.random.fold_in(stream_key, 6)
    for axis_at, parts in shards:
        steps = jnp.exp(jax.random.uniform(jax.random.fold_in(own, axis_at), (parts,), jnp.float32, smallest / len(shards), top_value / len(shards)))
        loudness = loudness * jnp.repeat(steps, shape[axis_at] // parts).reshape([-1 if axis == axis_at else 1 for axis in range(len(shape))])
    return loudness


def noise(rng, shape, spread, most, split=(), held_as=jnp.bfloat16):
    values = jax.random.normal(rng, shape, jnp.float32) * spread
    if len(split) > 0:
        values = block_levels(rng, shape, split, -0.22, 0.18) * values
    return jnp.clip(values, min=-most, max=most).astype(held_as)


def setup_inputs(seed: int = 0) -> dict:
    arg_keys = jax.random.split(jax.random.key(seed), 5)
    return {
        "history": noise(arg_keys[0], (2, TW, TW, N, N), 1.0, 6.0, ((1, 16), (2, 8)), jnp.float32),
        "self_energy": noise(arg_keys[1], (2, TW, N, N), 1.0, 6.0, ((1, 16),), jnp.float32),
        "green_row": noise(arg_keys[2], (2, TW, N, N), 1.0, 6.0, ((1, 8),), jnp.float32),
        "propagator": noise(arg_keys[3], (2, N, N), (2 * N) ** -0.5, 0.375, (), jnp.float32),
    }


COUPLING = 1.5
MIXING = 0.7


def complex_product(left, right, form):
    highest = lax.Precision.HIGHEST
    real_part = jnp.einsum(form, left[0], right[0], precision=highest) - jnp.einsum(form, left[1], right[1], precision=highest)
    imag_part = jnp.einsum(form, left[0], right[1], precision=highest) + jnp.einsum(form, left[1], right[0], precision=highest)
    return real_part, imag_part


def self_energy_of(green):
    modulus = green[0] * green[0] + green[1] * green[1]
    factor = -COUPLING * modulus / (1.0 + modulus)
    return jnp.stack([factor * green[0], factor * green[1]])


def collide(self_energy, history):
    norm_factor = float(TW * N) ** -0.5

    def block_terms(index):
        section = lax.dynamic_slice_in_dim(history, index * TT, TT, 2)
        real_part, imag_part = complex_product(self_energy, section, "sik,stkj->tij")
        return jnp.stack([real_part, imag_part]) * norm_factor

    blocks = lax.map(block_terms, jnp.arange(TW // TT, dtype=jnp.int32))
    return jnp.moveaxis(blocks, 0, 1).reshape(2, TW, N, N)


def reference(history, self_energy, green_row, propagator):
    new_rows = []
    for step_index in range(STEPS):
        collision = collide(self_energy, history)
        prop_real, prop_imag = complex_product(propagator, green_row, "ik,tkj->tij")
        green_row = jnp.stack([MIXING * (prop_real + collision[1]), MIXING * (prop_imag - collision[0])])
        new_rows.append(green_row)
        self_energy = self_energy_of(green_row)
        history = lax.dynamic_update_slice_in_dim(history, green_row[:, None], step_index * SH, 1)
    return jnp.stack(new_rows)
```

```python
import jax
import jax.numpy as jnp
import numpy as np
from jax import lax
from jax.sharding import PartitionSpec as P

STEPS = 4
COUPLING = 1.5
MIXING = 0.7
CHIPS = 8
CORES = 2
TGT = 8
HIST = CHIPS * CORES

ROUTE = np.array(
    [
        (4, 2, 0, 6, 5, 3, 1, 7),
        (3, 5, 7, 1, 2, 4, 6, 0),
        (2, 0, 6, 4, 3, 1, 7, 5),
        (1, 3, 5, 7, 0, 2, 4, 6),
        (1, 3, 5, 7, 0, 2, 4, 6),
        (2, 0, 6, 4, 3, 1, 7, 5),
        (7, 1, 3, 5, 6, 0, 2, 4),
        (0, 6, 4, 2, 1, 7, 5, 3),
    ],
    np.int32,
)
CHIP_GROUPS = [[CORES * w + c for w in range(CHIPS)] for c in range(CORES)]
PARTNER = [(h, h ^ 1) for h in range(HIST)]
TURN = [
    (a * HIST + h, int(ROUTE[a][h // CORES]) * HIST + CORES * a + h % CORES)
    for a in range(TGT)
    for h in range(HIST)
]


def complex_product(left, right, form):
    dot = lambda p, q: jnp.einsum(form, p, q, precision=lax.Precision.HIGH)
    return jnp.stack(
        [dot(left[0], right[0]) - dot(left[1], right[1]), dot(left[0], right[1]) + dot(left[1], right[0])]
    )


def self_energy_of(green):
    modulus = green[0] * green[0] + green[1] * green[1]
    factor = -COUPLING * modulus / (1.0 + modulus)
    return jnp.stack([factor * green[0], factor * green[1]])


def per_device(history, self_energy, green_row, propagator):
    _, local_s, local_t, n, _ = history.shape
    half_t = local_t // CORES
    band = n // CHIPS
    sub = band // CORES
    hist_index = lax.axis_index("hist")
    chip, core = hist_index // CORES, hist_index % CORES
    scale = MIXING * float(local_s * HIST * n) ** -0.5
    order = jnp.asarray(ROUTE)[chip]

    def turned(energy):
        return jnp.stack([scale * energy[1], -scale * energy[0]])

    rows_of = lambda value, axis: lax.dynamic_slice_in_dim(value, hist_index * sub, sub, axis)
    prop_cols = MIXING * rows_of(propagator, 2)
    energy = turned(self_energy)
    newest = rows_of(green_row, 2)
    slots, slot_rows, outs = [], [], []
    for step in range(STEPS):
        final_step = step == STEPS - 1
        left = [prop_cols] + slots
        right = [newest] + slot_rows
        part = complex_product(energy, history, "sik,stkj->tij")
        part = part + complex_product(
            jnp.concatenate(left, 2), jnp.concatenate(right, 2), "ik,tkj->tij"
        )
        part = part.reshape(2, CORES, half_t, n, n)
        mine = lax.dynamic_index_in_dim(part, core, 1, keepdims=False)
        theirs = lax.dynamic_index_in_dim(part, 1 - core, 1, keepdims=False)
        mine = mine + lax.ppermute(theirs, "hist", PARTNER)
        pieces = mine.reshape(2, half_t, CHIPS, band, n).transpose(2, 0, 1, 3, 4).reshape(CHIPS, -1, n)
        if not final_step:
            cols = mine[:, 0].swapaxes(1, 2).reshape(2, CHIPS, band, n).transpose(1, 0, 2, 3)
            pieces = jnp.concatenate([pieces, cols.reshape(CHIPS, -1, n)], 1)
        got = lax.all_to_all(pieces, "hist", 0, 0, axis_index_groups=CHIP_GROUPS)
        got = jnp.sum(got.reshape((CHIPS,) + pieces.shape[1:]), 0)
        main = got[: 2 * half_t * band]
        if not final_step:
            moved = lax.ppermute(main, ("tgt", "hist"), TURN)
        by_core = main.reshape(2, half_t, CORES, sub, n)
        keep = lax.dynamic_index_in_dim(by_core, core, 2, keepdims=False)
        send = lax.dynamic_index_in_dim(by_core, 1 - core, 2, keepdims=False).reshape(-1, n)
        if not final_step:
            cols = got[2 * half_t * band :].reshape(2, CORES, sub, n)
            keep_cols = lax.dynamic_index_in_dim(cols, core, 1, keepdims=False)
            send_cols = lax.dynamic_index_in_dim(cols, 1 - core, 1, keepdims=False)
            send = jnp.concatenate([send, send_cols.reshape(-1, n)], 0)
        other = lax.ppermute(send, "hist", PARTNER)
        other_rows = other[: 2 * half_t * sub].reshape(2, half_t, sub, n)
        newest = jnp.concatenate(
            [jnp.where(core == 0, keep, other_rows), jnp.where(core == 0, other_rows, keep)], 1
        )
        outs.append(newest)
        if final_step:
            break
        other_cols = other[2 * half_t * sub :].reshape(2, sub, n)
        cols = jnp.stack(
            [jnp.where(core == 0, keep_cols, other_cols), jnp.where(core == 0, other_cols, keep_cols)]
        )
        block = jnp.concatenate([moved, cols.reshape(-1, n)], 0)
        spread = lax.all_to_all(jnp.broadcast_to(block, (TGT,) + block.shape), "tgt", 0, 0)
        spread = spread.reshape((TGT,) + block.shape)
        rows = spread[:, : 2 * half_t * band].reshape(TGT, 2, half_t, band, n)[order]
        rows = rows.transpose(1, 2, 0, 3, 4).reshape(2, half_t, n, n)
        energy = turned(self_energy_of(rows))
        stale = hist_index <= step
        energy = energy.at[:, 0].set(jnp.where(stale, 0.0, energy[:, 0]))
        cols = spread[:, 2 * half_t * band :].reshape(TGT * CORES, 2, sub, n)
        slot_rows.append(newest)
        slots = [
            turned(self_energy_of(cols[m].swapaxes(1, 2))) for m in range(step + 1)
        ]
    return jnp.stack(outs)


def solution(mesh):
    in_specs = (
        P(None, "hist", "tgt", None, None),
        P(None, "hist", None, None),
        P(None, "tgt", None, None),
        P(),
    )
    out_specs = P(None, None, "tgt", "hist", None)
    return jax.shard_map(
        per_device, mesh=mesh, in_specs=in_specs, out_specs=out_specs, check_vma=False
    )
```

```python
import jax
import jax.numpy as jnp
import numpy as np
from jax import lax
from jax.experimental import pallas as pl
from jax.experimental.pallas import tpu as pltpu
from jax.sharding import PartitionSpec as P

STEPS = 4
COUPLING = 1.5
MIXING = 0.7
CHIPS = 8
CORES = 2
TGT = 8
HIST = CHIPS * CORES

ROUTE = np.array(
    [
        (4, 2, 0, 6, 5, 3, 1, 7),
        (3, 5, 7, 1, 2, 4, 6, 0),
        (2, 0, 6, 4, 3, 1, 7, 5),
        (1, 3, 5, 7, 0, 2, 4, 6),
        (1, 3, 5, 7, 0, 2, 4, 6),
        (2, 0, 6, 4, 3, 1, 7, 5),
        (7, 1, 3, 5, 6, 0, 2, 4),
        (0, 6, 4, 2, 1, 7, 5, 3),
    ],
    np.int32,
)
CHIP_GROUPS = [[CORES * w + c for w in range(CHIPS)] for c in range(CORES)]
PARTNER = [(h, h ^ 1) for h in range(HIST)]
TURN = [
    (a * HIST + h, int(ROUTE[a][h // CORES]) * HIST + CORES * a + h % CORES)
    for a in range(TGT)
    for h in range(HIST)
]


VMEM = pl.BlockSpec(memory_space=pltpu.VMEM)
SMEM = pl.BlockSpec(memory_space=pltpu.SMEM)
ANY = pl.BlockSpec(memory_space=pl.ANY)
F32 = jnp.float32
BF16 = jnp.bfloat16


def call(kernel, name, outs, specs, *args, scratch=(), limit=16):
    return pl.pallas_call(
        kernel,
        out_shape=outs,
        in_specs=specs,
        out_specs=[VMEM] * len(outs),
        scratch_shapes=scratch,
        compiler_params=pltpu.CompilerParams(vmem_limit_bytes=limit * 2**20),
        name=name,
    )(*args)


def saturated(real, imag):
    modulus = real * real + imag * imag
    factor = -COUPLING * modulus / (1.0 + modulus)
    return factor * real, factor * imag


def halves(value):
    high = value.astype(BF16)
    return high, (value - high.astype(F32)).astype(BF16)


def dot(left, right, at=1):
    return lax.dot_general(left, right, (((at,), (0,)), ((), ())), preferred_element_type=F32)


def wide(real, imag):
    return jnp.concatenate(
        [jnp.concatenate([real, -imag], 1), jnp.concatenate([imag, real], 1)], 0
    )


def side_terms(prop, cols, rows, slots, scale, half_t):
    sub = prop.shape[1]
    lefts = [(prop[0], prop[1])]
    for m in range(slots):
        real, imag = saturated(*cols(m))
        lefts.append((scale * imag, -scale * real))
    left = []
    for real, imag in lefts:
        left += [jnp.concatenate([real, imag], 1), jnp.concatenate([-imag, real], 1)]
    right = []
    for value in [rows[-1]] + list(rows[:slots]):
        for c in range(2):
            right.append(
                jnp.concatenate(
                    [value[(c * half_t + t) * sub : (c * half_t + t + 1) * sub] for t in range(half_t)], 1
                )
            )
    left_high, left_low = halves(jnp.concatenate(left, 0))
    right_high, right_low = halves(jnp.concatenate(right, 0))
    return dot(left_high, right_high, 0) + (dot(left_high, right_low, 0) + dot(left_low, right_high, 0))


def store_pieces(whole, out, half_t, n, band):
    for w in range(CHIPS):
        for c in range(2):
            for t in range(half_t):
                at = (c * half_t + t) * band
                out[w, at : at + band, :] = whole[
                    c * n + w * band : c * n + (w + 1) * band, t * n : (t + 1) * n
                ]


def collide_first(place, energy, history, prop, rows, scale):
    _, local_s, local_t, n, _ = history.shape
    half_t = local_t // CORES
    band = n // CHIPS

    def kernel(place, energy, history, prop, rows, out, split, fetched, arrived):
        copies = [
            pltpu.make_async_copy(
                history.at[:, s, pl.ds(place[0] * half_t, half_t)], fetched.at[s], arrived.at[s]
            )
            for s in range(local_s)
        ]
        for copy in copies:
            copy.start()
        total = side_terms(prop, None, [rows[...]], 0, scale, half_t)
        for s in range(local_s):
            left_high, left_low = halves(wide(scale * energy[1, s], -scale * energy[0, s]))
            copies[s].wait()
            right = jnp.concatenate(
                [jnp.concatenate([fetched[s, c, t] for t in range(half_t)], 1) for c in range(2)], 0
            )
            right_high, right_low = halves(right)
            at = slice(2 * n * s, 2 * n * (s + 1))
            split[0, at, :] = right_high
            split[1, at, :] = right_low
            total = total + dot(left_high, right_high)
            total = total + dot(left_high, right_low)
            total = total + dot(left_low, right_high)
        store_pieces(total, out, half_t, n, band)

    return call(
        kernel,
        "collide_first",
        [
            jax.ShapeDtypeStruct((CHIPS, 2 * half_t * band, n), F32),
            jax.ShapeDtypeStruct((2, 2 * n * local_s, half_t * n), BF16),
        ],
        [SMEM, VMEM, ANY, VMEM, VMEM],
        place,
        energy,
        history,
        prop,
        rows,
        scratch=[
            pltpu.VMEM((local_s, 2, half_t, n, n), F32),
            pltpu.SemaphoreType.DMA((local_s,)),
        ],
    )


def collide(place, spread, split, prop, rows, slots, scale, local_s, half_t):
    n = spread.shape[-1]
    band = n // CHIPS
    sub = band // CORES

    def kernel(place, spread, split, prop, *refs):
        rows, out = [ref[...] for ref in refs[:-1]], refs[-1]

        def cols(m):
            at = 2 * half_t * band + (m % 2) * 2 * sub
            return spread[m // 2, at : at + sub, :], spread[m // 2, at + sub : at + 2 * sub, :]

        highs, lows = [], []
        for s in range(local_s):
            real, imag = saturated(
                *(
                    jnp.concatenate(
                        [
                            spread[place[2 + w], (c * half_t + s) * band : (c * half_t + s + 1) * band, :]
                            for w in range(CHIPS)
                        ],
                        0,
                    )
                    for c in range(2)
                )
            )
            gain = scale if s else jnp.where(place[1] == 1, 0.0, scale)
            high, low = halves(wide(gain * imag, -gain * real))
            highs.append(high)
            lows.append(low)
        high, low = jnp.concatenate(highs, 1), jnp.concatenate(lows, 1)
        total = side_terms(prop, cols, rows, slots, scale, half_t)
        both = dot(jnp.concatenate([high, low], 0), split[0])
        total = total + dot(high, split[1])
        total = total + (both[: 2 * n] + both[2 * n :])
        store_pieces(total, out, half_t, n, band)

    return call(
        kernel,
        "collide",
        [jax.ShapeDtypeStruct((CHIPS, 2 * half_t * band, n), F32)],
        [SMEM, VMEM, VMEM, VMEM] + [VMEM] * len(rows),
        place,
        spread,
        split,
        prop,
        *rows,
    )[0]


def join(mine, other, band, half_t, columns):
    chips, depth, n = mine.shape

    def kernel(mine, other, out):
        both = mine[...] + other[...]
        out[:, :depth, :] = both
        for c in range(2 * columns):
            at = c * half_t * band
            tile = jnp.concatenate([both[w, at : at + band] for w in range(chips)], 0).T
            for w in range(chips):
                out[w, depth + c * band : depth + (c + 1) * band, :] = tile[w * band : (w + 1) * band]

    shape = (chips, depth + 2 * band * columns, n)
    return call(kernel, "join", [jax.ShapeDtypeStruct(shape, F32)], [VMEM, VMEM], mine, other)[0]


def add_up(place, got, sub, depth):
    _, tall, n = got.shape
    groups = tall // (CORES * sub)

    def kernel(place, got, main, keep, send, total):
        parts = [got[w] for w in range(CHIPS)]
        while len(parts) > 1:
            parts = [p + q for p, q in zip(parts[::2], parts[1::2])]
        total[...] = parts[0]
        main[...] = parts[0][:depth]
        other = place[0]
        for g in range(groups):
            at = pl.multiple_of(g * CORES * sub + (1 - other) * sub, sub)
            keep[g * sub : (g + 1) * sub, :] = total[pl.ds(at, sub), :]
            at = pl.multiple_of(g * CORES * sub + other * sub, sub)
            send[g * sub : (g + 1) * sub, :] = total[pl.ds(at, sub), :]

    part = jax.ShapeDtypeStruct((groups * sub, n), F32)
    return call(
        kernel,
        "add_up",
        [jax.ShapeDtypeStruct((depth, n), F32), part, part],
        [SMEM, VMEM],
        place,
        got,
        scratch=[pltpu.VMEM((tall, n), F32)],
    )


def copies(place, main, keep, swapped, rows_depth):
    depth, n = main.shape
    cols = keep.shape[0] - rows_depth

    def kernel(place, main, keep, swapped, out):
        other = place[0]
        near = pl.multiple_of(depth + (1 - other) * cols, cols)
        far = pl.multiple_of(depth + other * cols, cols)
        for a in range(TGT):
            out[a, :depth, :] = main[...]
            out[a, pl.ds(near, cols), :] = keep[rows_depth:, :]
            out[a, pl.ds(far, cols), :] = swapped[rows_depth:, :]

    shape = (TGT, depth + CORES * cols, n)
    return call(
        kernel, "copies", [jax.ShapeDtypeStruct(shape, F32)], [SMEM, VMEM, VMEM, VMEM],
        place, main, keep, swapped,
    )[0]


def per_device(history, self_energy, green_row, propagator):
    _, local_s, local_t, n, _ = history.shape
    half_t = local_t // CORES
    band = n // CHIPS
    sub = band // CORES
    depth = 2 * half_t * band
    rows_depth = 2 * half_t * sub
    hist_index = lax.axis_index("hist").astype(jnp.int32)
    chip, core = hist_index // CORES, hist_index % CORES
    scale = MIXING * float(local_s * HIST * n) ** -0.5
    order = jnp.asarray(ROUTE)[chip]

    rows_of = lambda value, axis: lax.dynamic_slice_in_dim(value, hist_index * sub, sub, axis)
    prop = MIXING * rows_of(propagator, 2).swapaxes(1, 2)
    start = rows_of(green_row, 2).reshape(2, CORES, half_t, sub, n)
    half_of = lambda which: lax.dynamic_index_in_dim(start, which, 1, keepdims=False).reshape(-1, n)
    places = [
        jnp.concatenate([jnp.stack([1 - core, (hist_index < step).astype(jnp.int32)]), order])
        for step in range(STEPS)
    ]
    kept, sent, outs = [], [], []
    for step in range(STEPS):
        final_step = step == STEPS - 1
        place = places[step]
        if step == 0:
            theirs, split_theirs = collide_first(
                place, self_energy, history, prop, half_of(1 - core), scale
            )
        else:
            theirs = collide(place, spread, split_theirs, prop, sent, step, scale, local_s, half_t)
        other = lax.ppermute(theirs, "hist", PARTNER)
        if step == 0:
            mine, split_mine = collide_first(
                jnp.stack([core, core]), self_energy, history, prop, half_of(core), scale
            )
        else:
            mine = collide(place, spread, split_mine, prop, kept, step, scale, local_s, half_t)
        pieces = join(mine, other, band, half_t, not final_step)
        got = lax.all_to_all(pieces, "hist", 0, 0, axis_index_groups=CHIP_GROUPS)
        main, keep, send = add_up(place, got.reshape(pieces.shape), sub, depth)
        if not final_step:
            moved = lax.ppermute(main, ("tgt", "hist"), TURN)
        swapped = lax.ppermute(send, "hist", PARTNER)
        kept.append(keep)
        sent.append(swapped)
        rows = [v[:rows_depth].reshape(2, half_t, sub, n) for v in (keep, swapped)]
        outs.append(
            jnp.concatenate(
                [jnp.where(core == 0, rows[0], rows[1]), jnp.where(core == 0, rows[1], rows[0])], 1
            )
        )
        if not final_step:
            spread = copies(place, moved, keep, swapped, rows_depth)
            spread = lax.all_to_all(spread, "tgt", 0, 0).reshape(spread.shape)
    return jnp.stack(outs)


def solution(mesh):
    in_specs = (
        P(None, "hist", "tgt", None, None),
        P(None, "hist", None, None),
        P(None, "tgt", None, None),
        P(),
    )
    out_specs = P(None, None, "tgt", "hist", None)
    return jax.shard_map(
        per_device, mesh=mesh, in_specs=in_specs, out_specs=out_specs, check_vma=False
    )
```

```python
import jax
import jax.numpy as jnp
import numpy as np
from jax import lax
from jax.experimental import pallas as pl
from jax.experimental.pallas import tpu as pltpu
from jax.sharding import PartitionSpec as P

STEPS = 4
COUPLING = 1.5
MIXING = 0.7
CHIPS = 8
CORES = 2
TGT = 8
HIST = CHIPS * CORES

ROUTE = np.array(
    [
        (4, 2, 0, 6, 5, 3, 1, 7),
        (3, 5, 7, 1, 2, 4, 6, 0),
        (2, 0, 6, 4, 3, 1, 7, 5),
        (1, 3, 5, 7, 0, 2, 4, 6),
        (1, 3, 5, 7, 0, 2, 4, 6),
        (2, 0, 6, 4, 3, 1, 7, 5),
        (7, 1, 3, 5, 6, 0, 2, 4),
        (0, 6, 4, 2, 1, 7, 5, 3),
    ],
    np.int32,
)
CHIP_GROUPS = [[CORES * w + c for w in range(CHIPS)] for c in range(CORES)]
PARTNER = [(h, h ^ 1) for h in range(HIST)]
TURN = [
    (a * HIST + h, int(ROUTE[a][h // CORES]) * HIST + CORES * a + h % CORES)
    for a in range(TGT)
    for h in range(HIST)
]


VMEM = pl.BlockSpec(memory_space=pltpu.VMEM)
SMEM = pl.BlockSpec(memory_space=pltpu.SMEM)
HBM = pl.BlockSpec(memory_space=pltpu.HBM)
F32 = jnp.float32
BF16 = jnp.bfloat16


def call(kernel, name, outs, specs, *args, scratch=(), limit=16):
    return pl.pallas_call(
        kernel,
        out_shape=outs,
        in_specs=specs,
        out_specs=[VMEM] * len(outs),
        scratch_shapes=scratch,
        compiler_params=pltpu.CompilerParams(vmem_limit_bytes=limit * 2**20),
        name=name,
    )(*args)


def saturated(real, imag):
    modulus = real * real + imag * imag
    factor = -COUPLING * modulus / (1.0 + modulus)
    return factor * real, factor * imag


def halves(value):
    high = value.astype(BF16)
    return high, (value - high.astype(F32)).astype(BF16)


def dot(left, right, at=1):
    return lax.dot_general(left, right, (((at,), (0,)), ((), ())), preferred_element_type=F32)


def wide(real, imag):
    return jnp.concatenate(
        [jnp.concatenate([real, -imag], 1), jnp.concatenate([imag, real], 1)], 0
    )


def side_terms(prop, cols, rows, slots, scale, half_t):
    sub = prop.shape[1]
    lefts = [(prop[0], prop[1])]
    for m in range(slots):
        real, imag = saturated(*cols(m))
        lefts.append((scale * imag, -scale * real))
    left = []
    for real, imag in lefts:
        left += [jnp.concatenate([real, imag], 1), jnp.concatenate([-imag, real], 1)]
    right = []
    for value in [rows[-1]] + list(rows[:slots]):
        for c in range(2):
            right.append(
                jnp.concatenate(
                    [value[(c * half_t + t) * sub : (c * half_t + t + 1) * sub] for t in range(half_t)], 1
                )
            )
    left_high, left_low = halves(jnp.concatenate(left, 0))
    right_high, right_low = halves(jnp.concatenate(right, 0))
    return dot(left_high, right_high, 0) + (dot(left_high, right_low, 0) + dot(left_low, right_high, 0))


def store_pieces(whole, out, half_t, n, band):
    for w in range(CHIPS):
        for c in range(2):
            for t in range(half_t):
                at = (c * half_t + t) * band
                out[w, at : at + band, :] = whole[
                    c * n + w * band : c * n + (w + 1) * band, t * n : (t + 1) * n
                ]


def collide_first(place, energy, history, propagator, green, scale, far):
    _, local_s, local_t, n, _ = history.shape
    half_t = local_t // CORES
    band = n // CHIPS
    sub = band // CORES

    def kernel(place, energy, history, prop, green, out, split, *rest):
        half = 1 - place[0] if far else place[0]
        if far:
            prop_band, fetched, lefts, rows, whole, turned, arrived = rest
        else:
            fetched, lefts, rows, arrived = rest
        copies = []
        for s in range(local_s):
            copies.append(pltpu.make_async_copy(energy.at[:, s], lefts.at[s], arrived.at[s, 0]))
            copies.append(
                pltpu.make_async_copy(
                    history.at[:, s, pl.ds(half * half_t, half_t)], fetched.at[s], arrived.at[s, 1]
                )
            )
        at = pl.multiple_of(place[1] * sub, sub)
        late = [
            pltpu.make_async_copy(
                green.at[:, pl.ds(half * half_t, half_t), pl.ds(at, sub)], rows, arrived.at[local_s, 0]
            )
        ]
        if far:
            late.append(pltpu.make_async_copy(prop, whole, arrived.at[local_s, 1]))
        for copy in copies + late:
            copy.start()
        total = jnp.zeros((2 * n, half_t * n), F32)
        for s in range(local_s):
            copies[2 * s].wait()
            left_high, left_low = halves(wide(scale * lefts[s, 1], -scale * lefts[s, 0]))
            copies[2 * s + 1].wait()
            right = jnp.concatenate(
                [jnp.concatenate([fetched[s, c, t] for t in range(half_t)], 1) for c in range(2)], 0
            )
            right_high, right_low = halves(right)
            rows_at = slice(2 * n * s, 2 * n * (s + 1))
            split[0, rows_at, :] = right_high
            split[1, rows_at, :] = right_low
            total = total + dot(left_high, right_high)
            total = total + dot(left_high, right_low)
            total = total + dot(left_low, right_high)
        for copy in late:
            copy.wait()
        if far:
            for c in range(2):
                turned[...] = MIXING * whole[c].T
                prop_band[c] = turned[pl.ds(at, sub), :]
            side = prop_band
        else:
            side = prop
        total = total + side_terms(
            side, None, [rows[...].reshape(2 * half_t * sub, n)], 0, scale, half_t
        )
        store_pieces(total, out, half_t, n, band)

    outs = [
        jax.ShapeDtypeStruct((CHIPS, 2 * half_t * band, n), F32),
        jax.ShapeDtypeStruct((2, 2 * n * local_s, half_t * n), BF16),
    ]
    scratch = [
        pltpu.VMEM((local_s, 2, half_t, n, n), F32),
        pltpu.VMEM((local_s, 2, n, n), F32),
        pltpu.VMEM((2, half_t, sub, n), F32),
    ]
    if far:
        outs.append(jax.ShapeDtypeStruct((2, sub, n), F32))
        scratch += [pltpu.VMEM((2, n, n), F32), pltpu.VMEM((n, n), F32)]
    scratch.append(pltpu.SemaphoreType.DMA((local_s + 1, 2)))
    return call(
        kernel,
        "collide_first",
        outs,
        [SMEM, HBM, HBM, HBM if far else VMEM, HBM],
        place,
        energy,
        history,
        propagator,
        green,
        scratch=scratch,
    )


def collide(place, spread, split, prop, rows, slots, scale, local_s, half_t):
    n = spread.shape[-1]
    band = n // CHIPS
    sub = band // CORES

    def kernel(place, spread, split, prop, *refs):
        rows, out = [ref[...] for ref in refs[:-1]], refs[-1]

        def cols(m):
            at = 2 * half_t * band + (m % 2) * 2 * sub
            return spread[m // 2, at : at + sub, :], spread[m // 2, at + sub : at + 2 * sub, :]

        highs, lows = [], []
        for s in range(local_s):
            real, imag = saturated(
                *(
                    jnp.concatenate(
                        [
                            spread[place[2 + w], (c * half_t + s) * band : (c * half_t + s + 1) * band, :]
                            for w in range(CHIPS)
                        ],
                        0,
                    )
                    for c in range(2)
                )
            )
            gain = scale if s else jnp.where(place[1] < slots, 0.0, scale)
            high, low = halves(wide(gain * imag, -gain * real))
            highs.append(high)
            lows.append(low)
        high, low = jnp.concatenate(highs, 1), jnp.concatenate(lows, 1)
        total = side_terms(prop, cols, rows, slots, scale, half_t)
        both = dot(jnp.concatenate([high, low], 0), split[0])
        total = total + dot(high, split[1])
        total = total + (both[: 2 * n] + both[2 * n :])
        store_pieces(total, out, half_t, n, band)

    return call(
        kernel,
        "collide",
        [jax.ShapeDtypeStruct((CHIPS, 2 * half_t * band, n), F32)],
        [SMEM, VMEM, VMEM, VMEM] + [VMEM] * len(rows),
        place,
        spread,
        split,
        prop,
        *rows,
    )[0]


def collide_last(place, spread, splits, prop, rows, slots, scale, local_s, half_t, far):
    n = spread.shape[-1]
    band = n // CHIPS
    sub = band // CORES
    local_t = CORES * half_t

    def kernel(place, spread, near_split, far_split, prop, *refs):
        near_rows, far_rows = refs[:slots], refs[slots : 2 * slots]
        out, side = refs[2 * slots :]
        near = place[0]
        pick = 1 - near if far else near

        def cols(m):
            at = 2 * half_t * band + (m % 2) * 2 * sub
            return spread[m // 2, at : at + sub, :], spread[m // 2, at + sub : at + 2 * sub, :]

        highs, lows = [], []
        for s in range(local_s):
            real, imag = saturated(
                *(
                    jnp.concatenate(
                        [
                            spread[
                                place[2 + w],
                                pl.ds(pl.multiple_of((c * half_t + s) * band + pick * sub, sub), sub),
                                :,
                            ]
                            for w in range(CHIPS)
                        ],
                        0,
                    )
                    for c in range(2)
                )
            )
            gain = scale if s else jnp.where(place[1] < slots, 0.0, scale)
            high, low = halves(wide(gain * imag, -gain * real))
            highs.append(high)
            lows.append(low)
        high, low = jnp.concatenate(highs, 1), jnp.concatenate(lows, 1)
        both = jnp.concatenate([high, low], 0)
        for half, split, rows in ((near, near_split, near_rows), (1 - near, far_split, far_rows)):
            side[...] = side_terms(prop, cols, [ref[...] for ref in rows], slots, scale, half_t)
            twice = dot(both, split[0])
            total = dot(high, split[1]) + (twice[:n] + twice[n:])
            for w in range(CHIPS):
                for c in range(2):
                    at = pl.multiple_of(c * n + w * band + pick * sub, sub)
                    rest = side[pl.ds(at, sub), :]
                    for t in range(half_t):
                        to = pl.multiple_of((c * local_t + half * half_t + t) * sub, sub)
                        out[w, pl.ds(to, sub), :] = (
                            rest[:, t * n : (t + 1) * n]
                            + total[
                                c * n // 2 + w * sub : c * n // 2 + (w + 1) * sub, t * n : (t + 1) * n
                            ]
                        )

    return call(
        kernel,
        "collide_last",
        [jax.ShapeDtypeStruct((CHIPS, 2 * local_t * sub, n), F32)],
        [SMEM] + [VMEM] * (4 + len(rows[0]) + len(rows[1])),
        place,
        spread,
        *splits,
        prop,
        *rows[0],
        *rows[1],
        scratch=[pltpu.VMEM((2 * n, half_t * n), F32)],
    )[0]


def join(mine, other, band, half_t, columns):
    chips, depth, n = mine.shape

    def kernel(mine, other, out):
        both = mine[...] + other[...]
        out[:, :depth, :] = both
        for c in range(2 * columns):
            at = c * half_t * band
            tile = jnp.concatenate([both[w, at : at + band] for w in range(chips)], 0).T
            for w in range(chips):
                out[w, depth + c * band : depth + (c + 1) * band, :] = tile[w * band : (w + 1) * band]

    shape = (chips, depth + 2 * band * columns, n)
    return call(kernel, "join", [jax.ShapeDtypeStruct(shape, F32)], [VMEM, VMEM], mine, other)[0]


def add_up(place, got, sub, depth):
    _, tall, n = got.shape
    groups = tall // (CORES * sub)

    def kernel(place, got, main, keep, send, total):
        parts = [got[w] for w in range(CHIPS)]
        while len(parts) > 1:
            parts = [p + q for p, q in zip(parts[::2], parts[1::2])]
        total[...] = parts[0]
        main[...] = parts[0][:depth]
        core = place[0]
        for g in range(groups):
            at = pl.multiple_of(g * CORES * sub + core * sub, sub)
            keep[g * sub : (g + 1) * sub, :] = total[pl.ds(at, sub), :]
            at = pl.multiple_of(g * CORES * sub + (1 - core) * sub, sub)
            send[g * sub : (g + 1) * sub, :] = total[pl.ds(at, sub), :]

    part = jax.ShapeDtypeStruct((groups * sub, n), F32)
    return call(
        kernel,
        "add_up",
        [jax.ShapeDtypeStruct((depth, n), F32), part, part],
        [SMEM, VMEM],
        place,
        got,
        scratch=[pltpu.VMEM((tall, n), F32)],
    )


def add_last(got, done):
    _, tall, n = got.shape
    steps = len(done) + 1

    def kernel(got, *refs):
        done, (out, total, sent) = refs[:-3], refs[-3:]
        moves = [
            pltpu.make_async_copy(ref, out.at[k], sent.at[k]) for k, ref in enumerate(done + (total,))
        ]
        for move in moves[:-1]:
            move.start()
        parts = [got[w] for w in range(CHIPS)]
        while len(parts) > 1:
            parts = [p + q for p, q in zip(parts[::2], parts[1::2])]
        total[...] = parts[0]
        moves[-1].start()
        for move in moves:
            move.wait()

    return pl.pallas_call(
        kernel,
        out_shape=jax.ShapeDtypeStruct((steps, tall, n), F32),
        in_specs=[VMEM] * steps,
        out_specs=HBM,
        scratch_shapes=[pltpu.VMEM((tall, n), F32), pltpu.SemaphoreType.DMA((steps,))],
        compiler_params=pltpu.CompilerParams(vmem_limit_bytes=16 * 2**20),
        name="add_last",
    )(got, *done)


def copies(place, main, keep, swapped, rows_depth):
    depth, n = main.shape
    cols = keep.shape[0] - rows_depth
    part = rows_depth // 2

    def kernel(place, main, keep, swapped, out, newest):
        core = place[0]
        for half, value in ((core, keep), (1 - core, swapped)):
            to = pl.multiple_of(depth + half * cols, cols)
            for a in range(TGT):
                out[a, pl.ds(to, cols), :] = value[rows_depth:, :]
            for c in range(2):
                to = pl.multiple_of((c * CORES + half) * part, part)
                newest[pl.ds(to, part), :] = value[c * part : (c + 1) * part, :]
        for a in range(TGT):
            out[a, :depth, :] = main[...]

    return call(
        kernel,
        "copies",
        [
            jax.ShapeDtypeStruct((TGT, depth + CORES * cols, n), F32),
            jax.ShapeDtypeStruct((CORES * rows_depth, n), F32),
        ],
        [SMEM, VMEM, VMEM, VMEM],
        place,
        main,
        keep,
        swapped,
    )


def per_device(history, self_energy, green_row, propagator):
    _, local_s, local_t, n, _ = history.shape
    half_t = local_t // CORES
    band = n // CHIPS
    sub = band // CORES
    depth = 2 * half_t * band
    rows_depth = 2 * half_t * sub
    in_hbm = lambda value: pltpu.with_memory_space_constraint(value, pltpu.HBM)
    history, self_energy, green_row, propagator = (
        in_hbm(value) for value in (history, self_energy, green_row, propagator)
    )
    hist_index = lax.axis_index("hist").astype(jnp.int32)
    chip, core = hist_index // CORES, hist_index % CORES
    scale = MIXING * float(local_s * HIST * n) ** -0.5
    order = jnp.asarray(ROUTE)[chip]

    place = jnp.concatenate([jnp.stack([core, hist_index]), order])
    kept, sent, outs = [], [], []
    for step in range(STEPS):
        final_step = step == STEPS - 1

        def sums(far):
            if step == 0:
                return collide_first(
                    place, self_energy, history, propagator if far else prop, green_row, scale, far
                )
            if final_step:
                return collide_last(
                    place, spread, splits, prop, (kept, sent), step, scale, local_s, half_t, far
                )
            return collide(
                place, spread, splits[far], prop, sent if far else kept, step, scale, local_s, half_t
            )

        if step == 0:
            theirs, split_far, prop = sums(True)
        else:
            theirs = sums(True)
        other = lax.ppermute(theirs, "hist", PARTNER)
        if step == 0:
            mine, split_near = sums(False)
            splits = (split_near, split_far)
        else:
            mine = sums(False)
        pieces = join(mine, other, band, half_t, not final_step)
        got = lax.all_to_all(pieces, "hist", 0, 0, axis_index_groups=CHIP_GROUPS)
        got = got.reshape(pieces.shape)
        if final_step:
            break
        main, keep, send = add_up(place, got, sub, depth)
        moved = lax.ppermute(main, ("tgt", "hist"), TURN)
        swapped = lax.ppermute(send, "hist", PARTNER)
        kept.append(keep)
        sent.append(swapped)
        spread, newest = copies(place, moved, keep, swapped, rows_depth)
        outs.append(newest)
        spread = lax.all_to_all(spread, "tgt", 0, 0).reshape(spread.shape)
    return add_last(got, outs).reshape(STEPS, 2, local_t, sub, n)


def solution(mesh):
    in_specs = (
        P(None, "hist", "tgt", None, None),
        P(None, "hist", None, None),
        P(None, "tgt", None, None),
        P(),
    )
    out_specs = P(None, None, "tgt", "hist", None)
    return jax.shard_map(
        per_device, mesh=mesh, in_specs=in_specs, out_specs=out_specs, check_vma=False
    )
```

```python
import jax
import jax.numpy as jnp
import numpy as np
from jax import lax
from jax.experimental import pallas as pl
from jax.experimental.pallas import tpu as pltpu
from jax.sharding import PartitionSpec as P

STEPS = 4
COUPLING = 1.5
MIXING = 0.7
CHIPS = 8
CORES = 2
TGT = 8
HIST = CHIPS * CORES

ROUTE = np.array(
    [
        (4, 2, 0, 6, 5, 3, 1, 7),
        (3, 5, 7, 1, 2, 4, 6, 0),
        (2, 0, 6, 4, 3, 1, 7, 5),
        (1, 3, 5, 7, 0, 2, 4, 6),
        (1, 3, 5, 7, 0, 2, 4, 6),
        (2, 0, 6, 4, 3, 1, 7, 5),
        (7, 1, 3, 5, 6, 0, 2, 4),
        (0, 6, 4, 2, 1, 7, 5, 3),
    ],
    np.int32,
)
ROUTE_BITS = [sum(int(ROUTE[x, w]) << (3 * x) for x in range(CHIPS)) for w in range(CHIPS)]
CHIP_GROUPS = [[CORES * w + c for w in range(CHIPS)] for c in range(CORES)]
PARTNER = [(h, h ^ 1) for h in range(HIST)]
TURN = [
    (a * HIST + h, int(ROUTE[a][h // CORES]) * HIST + CORES * a + h % CORES)
    for a in range(TGT)
    for h in range(HIST)
]


VMEM = pl.BlockSpec(memory_space=pltpu.VMEM)
HBM = pl.BlockSpec(memory_space=pltpu.HBM)
F32 = jnp.float32
BF16 = jnp.bfloat16


def call(kernel, name, outs, specs, *args, scratch=(), limit=16):
    return pl.pallas_call(
        kernel,
        out_shape=outs,
        in_specs=specs,
        out_specs=[VMEM] * len(outs),
        scratch_shapes=scratch,
        compiler_params=pltpu.CompilerParams(vmem_limit_bytes=limit * 2**20),
        name=name,
    )(*args)


def seat():
    index = lax.axis_index("hist").astype(jnp.int32)
    return index, index & (CORES - 1)


def route(index):
    shift = 3 * (index >> 1)
    return [(jnp.int32(bits) >> shift) & (TGT - 1) for bits in ROUTE_BITS]


def saturated(real, imag):
    modulus = real * real + imag * imag
    factor = -COUPLING * modulus / (1.0 + modulus)
    return factor * real, factor * imag


def halves(value):
    high = value.astype(BF16)
    return high, (value - high.astype(F32)).astype(BF16)


def dot(left, right, at=1):
    return lax.dot_general(left, right, (((at,), (0,)), ((), ())), preferred_element_type=F32)


def wide(real, imag):
    return jnp.concatenate(
        [jnp.concatenate([real, -imag], 1), jnp.concatenate([imag, real], 1)], 0
    )


def side_terms(prop, cols, rows, slots, scale, half_t):
    sub = prop.shape[1]
    lefts = [(prop[0], prop[1])]
    for m in range(slots):
        real, imag = saturated(*cols(m))
        lefts.append((scale * imag, -scale * real))
    left = []
    for real, imag in lefts:
        left += [jnp.concatenate([real, imag], 1), jnp.concatenate([-imag, real], 1)]
    right = []
    for value in [rows[-1]] + list(rows[:slots]):
        for c in range(2):
            right.append(
                jnp.concatenate(
                    [value[(c * half_t + t) * sub : (c * half_t + t + 1) * sub] for t in range(half_t)], 1
                )
            )
    left_high, left_low = halves(jnp.concatenate(left, 0))
    right_high, right_low = halves(jnp.concatenate(right, 0))
    return dot(left_high, right_high, 0) + (dot(left_high, right_low, 0) + dot(left_low, right_high, 0))


def store_pieces(whole, out, half_t, n, band):
    for w in range(CHIPS):
        for c in range(2):
            for t in range(half_t):
                at = (c * half_t + t) * band
                out[w, at : at + band, :] = whole[
                    c * n + w * band : c * n + (w + 1) * band, t * n : (t + 1) * n
                ]


def collide_first(energy, history, propagator, green, scale):
    _, local_s, local_t, n, _ = history.shape
    half_t = local_t // CORES
    band = n // CHIPS
    sub = band // CORES

    def kernel(
        energy, history, prop, green,
        out, far_split, near_split, lefts, near_rows, prop_band,
        far_fetched, near_fetched, far_rows, whole, turned, arrived,
    ):
        index, core = seat()
        at = pl.multiple_of(index * sub, sub)
        count = iter(range(3 * local_s + 3))
        move = lambda source, target: pltpu.make_async_copy(source, target, arrived.at[next(count)])
        span = lambda half: pl.ds(half * half_t, half_t)
        far, near, left_moves = [], [], []
        for s in range(local_s):
            left_moves.append(move(energy.at[:, s], lefts.at[s]))
            far.append(move(history.at[:, s, span(1 - core)], far_fetched.at[s]))
        side = [
            move(green.at[:, span(1 - core), pl.ds(at, sub)], far_rows),
            move(prop, whole),
        ]
        for s in range(local_s):
            near.append(move(history.at[:, s, span(core)], near_fetched.at[s]))
        late = move(green.at[:, span(core), pl.ds(at, sub)], near_rows)
        for pair in zip(left_moves, far):
            for copy in pair:
                copy.start()
        for copy in side + near + [late]:
            copy.start()

        def block(fetched, s):
            return halves(
                jnp.concatenate(
                    [jnp.concatenate([fetched[s, c, t] for t in range(half_t)], 1) for c in range(2)], 0
                )
            )

        total = jnp.zeros((2 * n, half_t * n), F32)
        for s in range(local_s):
            left_moves[s].wait()
            left_high, left_low = halves(wide(scale * lefts[s, 1], -scale * lefts[s, 0]))
            far[s].wait()
            right_high, right_low = block(far_fetched, s)
            rows_at = slice(2 * n * s, 2 * n * (s + 1))
            far_split[0, rows_at, :] = right_high
            far_split[1, rows_at, :] = right_low
            total = total + dot(left_high, right_high)
            total = total + dot(left_high, right_low)
            total = total + dot(left_low, right_high)
        for copy in side:
            copy.wait()
        for c in range(2):
            turned[...] = MIXING * whole[c].T
            prop_band[c] = turned[pl.ds(at, sub), :]
        total = total + side_terms(
            prop_band, None, [far_rows[...].reshape(2 * half_t * sub, n)], 0, scale, half_t
        )
        store_pieces(total, out, half_t, n, band)
        for s in range(local_s):
            near[s].wait()
            rows_at = slice(2 * n * s, 2 * n * (s + 1))
            near_split[0, rows_at, :], near_split[1, rows_at, :] = block(near_fetched, s)
        late.wait()

    split = jax.ShapeDtypeStruct((2, 2 * n * local_s, half_t * n), BF16)
    fetched = pltpu.VMEM((local_s, 2, half_t, n, n), F32)
    return call(
        kernel,
        "collide_first",
        [
            jax.ShapeDtypeStruct((CHIPS, 2 * half_t * band, n), F32),
            split,
            split,
            jax.ShapeDtypeStruct((local_s, 2, n, n), F32),
            jax.ShapeDtypeStruct((2, half_t, sub, n), F32),
            jax.ShapeDtypeStruct((2, sub, n), F32),
        ],
        [HBM] * 4,
        energy,
        history,
        propagator,
        green,
        scratch=[
            fetched,
            fetched,
            pltpu.VMEM((2, half_t, sub, n), F32),
            pltpu.VMEM((2, n, n), F32),
            pltpu.VMEM((n, n), F32),
            pltpu.SemaphoreType.DMA((3 * local_s + 3,)),
        ],
    )


def slot_cols(spread, m, half_t, band, sub):
    at = 2 * half_t * band + (m % 2) * 2 * sub
    return spread[m // 2, at : at + sub, :], spread[m // 2, at + sub : at + 2 * sub, :]


def collide(spread, split, prop, rows, slots, scale, local_s, half_t):
    n = spread.shape[-1]
    band = n // CHIPS
    sub = band // CORES

    def kernel(spread, split, prop, *refs):
        rows, out = [ref[...] for ref in refs[:-1]], refs[-1]
        index, _ = seat()
        order = route(index)
        highs, lows = [], []
        for s in range(local_s):
            if slots == 0:
                real, imag = spread[s, 0], spread[s, 1]
            else:
                real, imag = saturated(
                    *(
                        jnp.concatenate(
                            [
                                spread[
                                    order[w], (c * half_t + s) * band : (c * half_t + s + 1) * band, :
                                ]
                                for w in range(CHIPS)
                            ],
                            0,
                        )
                        for c in range(2)
                    )
                )
            gain = scale if s or not slots else jnp.where(index < slots, 0.0, scale)
            high, low = halves(wide(gain * imag, -gain * real))
            highs.append(high)
            lows.append(low)
        high, low = jnp.concatenate(highs, 1), jnp.concatenate(lows, 1)
        cols = lambda m: slot_cols(spread, m, half_t, band, sub)
        total = side_terms(prop, cols, rows, slots, scale, half_t)
        both = dot(jnp.concatenate([high, low], 0), split[0])
        total = total + dot(high, split[1])
        total = total + (both[: 2 * n] + both[2 * n :])
        store_pieces(total, out, half_t, n, band)

    return call(
        kernel,
        "collide",
        [jax.ShapeDtypeStruct((CHIPS, 2 * half_t * band, n), F32)],
        [VMEM] * (3 + len(rows)),
        spread,
        split,
        prop,
        *rows,
    )[0]


def collide_last(spread, splits, prop, rows, slots, scale, local_s, half_t, far):
    n = spread.shape[-1]
    band = n // CHIPS
    sub = band // CORES
    local_t = CORES * half_t

    def kernel(spread, near_split, far_split, prop, *refs):
        near_rows, far_rows = refs[:slots], refs[slots : 2 * slots]
        out, side = refs[2 * slots :]
        index, near = seat()
        order = route(index)
        pick = 1 - near if far else near
        cols = lambda m: slot_cols(spread, m, half_t, band, sub)
        highs, lows = [], []
        for s in range(local_s):
            real, imag = saturated(
                *(
                    jnp.concatenate(
                        [
                            spread[
                                order[w],
                                pl.ds(pl.multiple_of((c * half_t + s) * band + pick * sub, sub), sub),
                                :,
                            ]
                            for w in range(CHIPS)
                        ],
                        0,
                    )
                    for c in range(2)
                )
            )
            gain = scale if s else jnp.where(index < slots, 0.0, scale)
            high, low = halves(wide(gain * imag, -gain * real))
            highs.append(high)
            lows.append(low)
        high, low = jnp.concatenate(highs, 1), jnp.concatenate(lows, 1)
        both = jnp.concatenate([high, low], 0)
        for half, split, rows in ((near, near_split, near_rows), (1 - near, far_split, far_rows)):
            side[...] = side_terms(prop, cols, [ref[...] for ref in rows], slots, scale, half_t)
            twice = dot(both, split[0])
            total = dot(high, split[1]) + (twice[:n] + twice[n:])
            for w in range(CHIPS):
                for c in range(2):
                    at = pl.multiple_of(c * n + w * band + pick * sub, sub)
                    rest = side[pl.ds(at, sub), :]
                    for t in range(half_t):
                        to = pl.multiple_of((c * local_t + half * half_t + t) * sub, sub)
                        out[w, pl.ds(to, sub), :] = (
                            rest[:, t * n : (t + 1) * n]
                            + total[
                                c * n // 2 + w * sub : c * n // 2 + (w + 1) * sub, t * n : (t + 1) * n
                            ]
                        )

    return call(
        kernel,
        "collide_last",
        [jax.ShapeDtypeStruct((CHIPS, 2 * local_t * sub, n), F32)],
        [VMEM] * (4 + len(rows[0]) + len(rows[1])),
        spread,
        *splits,
        prop,
        *rows[0],
        *rows[1],
        scratch=[pltpu.VMEM((2 * n, half_t * n), F32)],
    )[0]


def join(mine, other, band, half_t, columns):
    chips, depth, n = mine.shape

    def kernel(mine, other, out):
        both = mine[...] + other[...]
        out[:, :depth, :] = both
        for c in range(2 * columns):
            at = c * half_t * band
            tile = jnp.concatenate([both[w, at : at + band] for w in range(chips)], 0).T
            for w in range(chips):
                out[w, depth + c * band : depth + (c + 1) * band, :] = tile[w * band : (w + 1) * band]

    shape = (chips, depth + 2 * band * columns, n)
    return call(kernel, "join", [jax.ShapeDtypeStruct(shape, F32)], [VMEM, VMEM], mine, other)[0]


def add_up(got, sub, depth):
    _, tall, n = got.shape
    groups = tall // (CORES * sub)

    def kernel(got, main, keep, send, total):
        parts = [got[w] for w in range(CHIPS)]
        while len(parts) > 1:
            parts = [p + q for p, q in zip(parts[::2], parts[1::2])]
        total[...] = parts[0]
        main[...] = parts[0][:depth]
        _, core = seat()
        for g in range(groups):
            at = pl.multiple_of(g * CORES * sub + core * sub, sub)
            keep[g * sub : (g + 1) * sub, :] = total[pl.ds(at, sub), :]
            at = pl.multiple_of(g * CORES * sub + (1 - core) * sub, sub)
            send[g * sub : (g + 1) * sub, :] = total[pl.ds(at, sub), :]

    part = jax.ShapeDtypeStruct((groups * sub, n), F32)
    return call(
        kernel,
        "add_up",
        [jax.ShapeDtypeStruct((depth, n), F32), part, part],
        [VMEM],
        got,
        scratch=[pltpu.VMEM((tall, n), F32)],
    )


def add_last(got, done):
    _, tall, n = got.shape
    steps = len(done) + 1

    def kernel(got, *refs):
        done, (out, total, sent) = refs[:-3], refs[-3:]
        moves = [
            pltpu.make_async_copy(ref, out.at[k], sent.at[k]) for k, ref in enumerate(done + (total,))
        ]
        for move in moves[:-1]:
            move.start()
        parts = [got[w] for w in range(CHIPS)]
        while len(parts) > 1:
            parts = [p + q for p, q in zip(parts[::2], parts[1::2])]
        total[...] = parts[0]
        moves[-1].start()
        for move in moves:
            move.wait()

    return pl.pallas_call(
        kernel,
        out_shape=jax.ShapeDtypeStruct((steps, tall, n), F32),
        in_specs=[VMEM] * steps,
        out_specs=HBM,
        scratch_shapes=[pltpu.VMEM((tall, n), F32), pltpu.SemaphoreType.DMA((steps,))],
        compiler_params=pltpu.CompilerParams(vmem_limit_bytes=16 * 2**20),
        name="add_last",
    )(got, *done)


def copies(main, keep, swapped, rows_depth, shares):
    depth, n = main.shape
    cols = keep.shape[0] - rows_depth
    part = rows_depth // 2

    def kernel(main, keep, swapped, out, newest):
        _, core = seat()
        for half, value in ((core, keep), (1 - core, swapped)):
            if shares == CORES:
                to = pl.multiple_of(depth + half * cols, cols)
                for a in range(TGT):
                    out[a, pl.ds(to, cols), :] = value[rows_depth:, :]
            for c in range(2):
                to = pl.multiple_of((c * CORES + half) * part, part)
                newest[pl.ds(to, part), :] = value[c * part : (c + 1) * part, :]
        if shares == 1:
            only = jnp.where(core == 0, keep[rows_depth:, :], swapped[rows_depth:, :])
            for a in range(TGT):
                out[a, depth:, :] = only
        for a in range(TGT):
            out[a, :depth, :] = main[...]

    return call(
        kernel,
        "copies",
        [
            jax.ShapeDtypeStruct((TGT, depth + shares * cols, n), F32),
            jax.ShapeDtypeStruct((CORES * rows_depth, n), F32),
        ],
        [VMEM] * 3,
        main,
        keep,
        swapped,
    )


def per_device(history, self_energy, green_row, propagator):
    _, local_s, local_t, n, _ = history.shape
    half_t = local_t // CORES
    band = n // CHIPS
    sub = band // CORES
    depth = 2 * half_t * band
    rows_depth = 2 * half_t * sub
    in_hbm = lambda value: pltpu.with_memory_space_constraint(value, pltpu.HBM)
    history, self_energy, green_row, propagator = (
        in_hbm(value) for value in (history, self_energy, green_row, propagator)
    )
    scale = MIXING * float(local_s * HIST * n) ** -0.5
    theirs, far_split, near_split, energy, near_rows, prop = collide_first(
        self_energy, history, propagator, green_row, scale
    )
    splits = (near_split, far_split)
    kept, sent, outs = [near_rows.reshape(rows_depth, n)], [], []
    spread = energy
    for step in range(STEPS):
        final_step = step == STEPS - 1

        def sums(far):
            if final_step:
                return collide_last(
                    spread, splits, prop, (kept, sent), step, scale, local_s, half_t, far
                )
            rows = sent if far else kept
            return collide(spread, splits[far], prop, rows, step, scale, local_s, half_t)

        if step:
            theirs = sums(True)
        other = lax.ppermute(theirs, "hist", PARTNER)
        mine = sums(False)
        pieces = join(mine, other, band, half_t, not final_step)
        got = lax.all_to_all(pieces, "hist", 0, 0, axis_index_groups=CHIP_GROUPS)
        got = got.reshape(pieces.shape)
        if final_step:
            break
        main, keep, send = add_up(got, sub, depth)
        moved = lax.ppermute(main, ("tgt", "hist"), TURN)
        swapped = lax.ppermute(send, "hist", PARTNER)
        kept = (kept if step else []) + [keep]
        sent = sent + [swapped]
        spread, newest = copies(moved, keep, swapped, rows_depth, min(step + 1, CORES))
        outs.append(newest)
        spread = lax.all_to_all(spread, "tgt", 0, 0).reshape(spread.shape)
    return add_last(got, outs).reshape(STEPS, 2, local_t, sub, n)


def solution(mesh):
    in_specs = (
        P(None, "hist", "tgt", None, None),
        P(None, "hist", None, None),
        P(None, "tgt", None, None),
        P(),
    )
    out_specs = P(None, None, "tgt", "hist", None)
    return jax.shard_map(
        per_device, mesh=mesh, in_specs=in_specs, out_specs=out_specs, check_vma=False
    )
```

```python
import jax
import jax.numpy as jnp
import numpy as np
from jax import lax
from jax.experimental import pallas as pl
from jax.experimental.pallas import tpu as pltpu
from jax.sharding import PartitionSpec as P

STEPS = 4
COUPLING = 1.5
MIXING = 0.7
CHIPS = 8
CORES = 2
TGT = 8
HIST = CHIPS * CORES

ROUTE = np.array(
    [
        (4, 6, 0, 2, 5, 7, 1, 3),
        (5, 4, 7, 3, 1, 6, 2, 0),
        (2, 0, 6, 4, 3, 1, 7, 5),
        (1, 5, 7, 6, 3, 2, 0, 4),
        (3, 7, 5, 4, 1, 0, 2, 6),
        (2, 0, 6, 4, 3, 1, 7, 5),
        (7, 5, 1, 6, 4, 0, 3, 2),
        (4, 6, 0, 2, 5, 7, 1, 3),
    ],
    np.int32,
)
CHIP_ORDER = ((0, 5, 2, 7, 4, 1, 6, 3), (3, 6, 1, 4, 7, 2, 5, 0))
TGT_ORDER = ((0, 1, 3, 2, 4, 5, 7, 6), (0, 1, 3, 2, 4, 5, 7, 6))
CHIP_GROUPS = [[CORES * w + c for w in CHIP_ORDER[c]] for c in range(CORES)]
TGT_GROUPS = [
    [a * HIST + CORES * w + c for a in TGT_ORDER[c]] for w in range(CHIPS) for c in range(CORES)
]
ROUTE_BITS = [
    [sum(TGT_ORDER[c].index(int(ROUTE[x, w])) << (3 * x) for x in range(CHIPS)) for c in range(CORES)]
    for w in range(CHIPS)
]
PARTNER = [(h, h ^ 1) for h in range(HIST)]
TURN = [
    (a * HIST + h, int(ROUTE[a][h // CORES]) * HIST + CORES * a + h % CORES)
    for a in range(TGT)
    for h in range(HIST)
]


VMEM = pl.BlockSpec(memory_space=pltpu.VMEM)
HBM = pl.BlockSpec(memory_space=pltpu.HBM)
F32 = jnp.float32
BF16 = jnp.bfloat16


def call(kernel, name, outs, specs, *args, scratch=(), limit=16):
    return pl.pallas_call(
        kernel,
        out_shape=outs,
        in_specs=specs,
        out_specs=[VMEM] * len(outs),
        scratch_shapes=scratch,
        compiler_params=pltpu.CompilerParams(vmem_limit_bytes=limit * 2**20),
        name=name,
    )(*args)


def seat():
    index = lax.axis_index("hist").astype(jnp.int32)
    return index, index & (CORES - 1)


def of_core(core, choices):
    even, odd = choices
    return even if even == odd else jnp.where(core == 0, jnp.int32(even), jnp.int32(odd))


def route(index, core):
    shift = 3 * (index >> 1)
    return [(jnp.int32(of_core(core, bits)) >> shift) & (TGT - 1) for bits in ROUTE_BITS]


def saturated(real, imag):
    modulus = real * real + imag * imag
    factor = -COUPLING * modulus / (1.0 + modulus)
    return factor * real, factor * imag


def halves(value):
    high = value.astype(BF16)
    return high, (value - high.astype(F32)).astype(BF16)


def dot(left, right, at=1):
    return lax.dot_general(left, right, (((at,), (0,)), ((), ())), preferred_element_type=F32)


def wide(real, imag):
    return jnp.concatenate(
        [jnp.concatenate([real, -imag], 1), jnp.concatenate([imag, real], 1)], 0
    )


def side_terms(prop, cols, rows, slots, scale, half_t):
    sub = prop.shape[1]
    lefts = [(prop[0], prop[1])]
    for m in range(slots):
        real, imag = saturated(*cols(m))
        lefts.append((scale * imag, -scale * real))
    left = []
    for real, imag in lefts:
        left += [jnp.concatenate([real, imag], 1), jnp.concatenate([-imag, real], 1)]
    right = []
    for value in [rows[-1]] + list(rows[:slots]):
        for c in range(2):
            right.append(
                jnp.concatenate(
                    [value[(c * half_t + t) * sub : (c * half_t + t + 1) * sub] for t in range(half_t)], 1
                )
            )
    left_high, left_low = halves(jnp.concatenate(left, 0))
    right_high, right_low = halves(jnp.concatenate(right, 0))
    return dot(left_high, right_high, 0) + (dot(left_high, right_low, 0) + dot(left_low, right_high, 0))


def store_pieces(whole, out, half_t, n, band):
    for w in range(CHIPS):
        for c in range(2):
            for t in range(half_t):
                at = (c * half_t + t) * band
                out[w, at : at + band, :] = whole[
                    c * n + w * band : c * n + (w + 1) * band, t * n : (t + 1) * n
                ]


def collide_first(energy, history, propagator, green, scale):
    _, local_s, local_t, n, _ = history.shape
    half_t = local_t // CORES
    band = n // CHIPS
    sub = band // CORES

    def kernel(
        energy, history, prop, green,
        out, far_split, near_split, lefts, near_rows, prop_band,
        far_fetched, near_fetched, far_rows, whole, turned, arrived,
    ):
        index, core = seat()
        at = pl.multiple_of(index * sub, sub)
        count = iter(range(3 * local_s + 3))
        move = lambda source, target: pltpu.make_async_copy(source, target, arrived.at[next(count)])
        span = lambda half: pl.ds(half * half_t, half_t)
        far, near, left_moves = [], [], []
        for s in range(local_s):
            left_moves.append(move(energy.at[:, s], lefts.at[s]))
            far.append(move(history.at[:, s, span(1 - core)], far_fetched.at[s]))
        side = [
            move(green.at[:, span(1 - core), pl.ds(at, sub)], far_rows),
            move(prop, whole),
        ]
        for s in range(local_s):
            near.append(move(history.at[:, s, span(core)], near_fetched.at[s]))
        late = move(green.at[:, span(core), pl.ds(at, sub)], near_rows)
        for pair in zip(left_moves, far):
            for copy in pair:
                copy.start()
        for copy in side + near + [late]:
            copy.start()

        def block(fetched, s):
            return halves(
                jnp.concatenate(
                    [jnp.concatenate([fetched[s, c, t] for t in range(half_t)], 1) for c in range(2)], 0
                )
            )

        total = jnp.zeros((2 * n, half_t * n), F32)
        for s in range(local_s):
            left_moves[s].wait()
            left_high, left_low = halves(wide(scale * lefts[s, 1], -scale * lefts[s, 0]))
            far[s].wait()
            right_high, right_low = block(far_fetched, s)
            rows_at = slice(2 * n * s, 2 * n * (s + 1))
            far_split[0, rows_at, :] = right_high
            far_split[1, rows_at, :] = right_low
            total = total + dot(left_high, right_high)
            total = total + dot(left_high, right_low)
            total = total + dot(left_low, right_high)
        for copy in side:
            copy.wait()
        for c in range(2):
            turned[...] = MIXING * whole[c].T
            prop_band[c] = turned[pl.ds(at, sub), :]
        total = total + side_terms(
            prop_band, None, [far_rows[...].reshape(2 * half_t * sub, n)], 0, scale, half_t
        )
        store_pieces(total, out, half_t, n, band)
        for s in range(local_s):
            near[s].wait()
            rows_at = slice(2 * n * s, 2 * n * (s + 1))
            near_split[0, rows_at, :], near_split[1, rows_at, :] = block(near_fetched, s)
        late.wait()

    split = jax.ShapeDtypeStruct((2, 2 * n * local_s, half_t * n), BF16)
    fetched = pltpu.VMEM((local_s, 2, half_t, n, n), F32)
    return call(
        kernel,
        "collide_first",
        [
            jax.ShapeDtypeStruct((CHIPS, 2 * half_t * band, n), F32),
            split,
            split,
            jax.ShapeDtypeStruct((local_s, 2, n, n), F32),
            jax.ShapeDtypeStruct((2, half_t, sub, n), F32),
            jax.ShapeDtypeStruct((2, sub, n), F32),
        ],
        [HBM] * 4,
        energy,
        history,
        propagator,
        green,
        scratch=[
            fetched,
            fetched,
            pltpu.VMEM((2, half_t, sub, n), F32),
            pltpu.VMEM((2, n, n), F32),
            pltpu.VMEM((n, n), F32),
            pltpu.SemaphoreType.DMA((3 * local_s + 3,)),
        ],
    )


def slot_cols(spread, core, m, half_t, band, sub):
    a = of_core(core, [order.index(m // 2) for order in TGT_ORDER])
    at = 2 * half_t * band + (m % 2) * 2 * sub
    return spread[a, at : at + sub, :], spread[a, at + sub : at + 2 * sub, :]


def collide(spread, split, prop, rows, slots, scale, local_s, half_t):
    n = spread.shape[-1]
    band = n // CHIPS
    sub = band // CORES

    def kernel(spread, split, prop, *refs):
        rows, out = [ref[...] for ref in refs[:-1]], refs[-1]
        index, core = seat()
        order = route(index, core)
        highs, lows = [], []
        for s in range(local_s):
            if slots == 0:
                real, imag = spread[s, 0], spread[s, 1]
            else:
                real, imag = saturated(
                    *(
                        jnp.concatenate(
                            [
                                spread[
                                    order[w], (c * half_t + s) * band : (c * half_t + s + 1) * band, :
                                ]
                                for w in range(CHIPS)
                            ],
                            0,
                        )
                        for c in range(2)
                    )
                )
            gain = scale if s or not slots else jnp.where(index < slots, 0.0, scale)
            high, low = halves(wide(gain * imag, -gain * real))
            highs.append(high)
            lows.append(low)
        high, low = jnp.concatenate(highs, 1), jnp.concatenate(lows, 1)
        cols = lambda m: slot_cols(spread, core, m, half_t, band, sub)
        total = side_terms(prop, cols, rows, slots, scale, half_t)
        both = dot(jnp.concatenate([high, low], 0), split[0])
        total = total + dot(high, split[1])
        total = total + (both[: 2 * n] + both[2 * n :])
        store_pieces(total, out, half_t, n, band)

    return call(
        kernel,
        "collide",
        [jax.ShapeDtypeStruct((CHIPS, 2 * half_t * band, n), F32)],
        [VMEM] * (3 + len(rows)),
        spread,
        split,
        prop,
        *rows,
    )[0]


def collide_last(spread, splits, prop, rows, slots, scale, local_s, half_t, far):
    n = spread.shape[-1]
    band = n // CHIPS
    sub = band // CORES
    local_t = CORES * half_t

    def kernel(spread, near_split, far_split, prop, *refs):
        near_rows, far_rows = refs[:slots], refs[slots : 2 * slots]
        out, side = refs[2 * slots :]
        index, near = seat()
        order = route(index, near)
        pick = 1 - near if far else near
        cols = lambda m: slot_cols(spread, near, m, half_t, band, sub)
        highs, lows = [], []
        for s in range(local_s):
            real, imag = saturated(
                *(
                    jnp.concatenate(
                        [
                            spread[
                                order[w],
                                pl.ds(pl.multiple_of((c * half_t + s) * band + pick * sub, sub), sub),
                                :,
                            ]
                            for w in range(CHIPS)
                        ],
                        0,
                    )
                    for c in range(2)
                )
            )
            gain = scale if s else jnp.where(index < slots, 0.0, scale)
            high, low = halves(wide(gain * imag, -gain * real))
            highs.append(high)
            lows.append(low)
        high, low = jnp.concatenate(highs, 1), jnp.concatenate(lows, 1)
        both = jnp.concatenate([high, low], 0)
        for half, split, rows in ((near, near_split, near_rows), (1 - near, far_split, far_rows)):
            side[...] = side_terms(prop, cols, [ref[...] for ref in rows], slots, scale, half_t)
            twice = dot(both, split[0])
            total = dot(high, split[1]) + (twice[:n] + twice[n:])
            for w in range(CHIPS):
                for c in range(2):
                    at = pl.multiple_of(c * n + w * band + pick * sub, sub)
                    rest = side[pl.ds(at, sub), :]
                    for t in range(half_t):
                        to = pl.multiple_of((c * local_t + half * half_t + t) * sub, sub)
                        out[w, pl.ds(to, sub), :] = (
                            rest[:, t * n : (t + 1) * n]
                            + total[
                                c * n // 2 + w * sub : c * n // 2 + (w + 1) * sub, t * n : (t + 1) * n
                            ]
                        )

    return call(
        kernel,
        "collide_last",
        [jax.ShapeDtypeStruct((CHIPS, 2 * local_t * sub, n), F32)],
        [VMEM] * (4 + len(rows[0]) + len(rows[1])),
        spread,
        *splits,
        prop,
        *rows[0],
        *rows[1],
        scratch=[pltpu.VMEM((2 * n, half_t * n), F32)],
    )[0]


def join(mine, other, band, half_t, columns):
    chips, depth, n = mine.shape

    def kernel(mine, other, out):
        _, core = seat()
        slots = [of_core(core, [order.index(w) for order in CHIP_ORDER]) for w in range(chips)]
        both = mine[...] + other[...]
        for w in range(chips):
            out[slots[w], :depth, :] = both[w]
        for c in range(2 * columns):
            at = c * half_t * band
            tile = jnp.concatenate([both[w, at : at + band] for w in range(chips)], 0).T
            for w in range(chips):
                out[slots[w], depth + c * band : depth + (c + 1) * band, :] = tile[
                    w * band : (w + 1) * band
                ]

    shape = (chips, depth + 2 * band * columns, n)
    return call(kernel, "join", [jax.ShapeDtypeStruct(shape, F32)], [VMEM, VMEM], mine, other)[0]


def add_up(got, sub, depth):
    _, tall, n = got.shape
    groups = tall // (CORES * sub)

    def kernel(got, main, keep, send, total):
        parts = [got[w] for w in range(CHIPS)]
        while len(parts) > 1:
            parts = [p + q for p, q in zip(parts[::2], parts[1::2])]
        total[...] = parts[0]
        main[...] = parts[0][:depth]
        _, core = seat()
        for g in range(groups):
            at = pl.multiple_of(g * CORES * sub + core * sub, sub)
            keep[g * sub : (g + 1) * sub, :] = total[pl.ds(at, sub), :]
            at = pl.multiple_of(g * CORES * sub + (1 - core) * sub, sub)
            send[g * sub : (g + 1) * sub, :] = total[pl.ds(at, sub), :]

    part = jax.ShapeDtypeStruct((groups * sub, n), F32)
    return call(
        kernel,
        "add_up",
        [jax.ShapeDtypeStruct((depth, n), F32), part, part],
        [VMEM],
        got,
        scratch=[pltpu.VMEM((tall, n), F32)],
    )


def add_last(got, done):
    _, tall, n = got.shape
    steps = len(done) + 1

    def kernel(got, *refs):
        done, (out, total, sent) = refs[:-3], refs[-3:]
        moves = [
            pltpu.make_async_copy(ref, out.at[k], sent.at[k]) for k, ref in enumerate(done + (total,))
        ]
        for move in moves[:-1]:
            move.start()
        parts = [got[w] for w in range(CHIPS)]
        while len(parts) > 1:
            parts = [p + q for p, q in zip(parts[::2], parts[1::2])]
        total[...] = parts[0]
        moves[-1].start()
        for move in moves:
            move.wait()

    return pl.pallas_call(
        kernel,
        out_shape=jax.ShapeDtypeStruct((steps, tall, n), F32),
        in_specs=[VMEM] * steps,
        out_specs=HBM,
        scratch_shapes=[pltpu.VMEM((tall, n), F32), pltpu.SemaphoreType.DMA((steps,))],
        compiler_params=pltpu.CompilerParams(vmem_limit_bytes=16 * 2**20),
        name="add_last",
    )(got, *done)


def copies(main, keep, swapped, rows_depth, shares):
    depth, n = main.shape
    cols = keep.shape[0] - rows_depth
    part = rows_depth // 2

    def kernel(main, keep, swapped, out, newest):
        _, core = seat()
        for half, value in ((core, keep), (1 - core, swapped)):
            if shares == CORES:
                to = pl.multiple_of(depth + half * cols, cols)
                for a in range(TGT):
                    out[a, pl.ds(to, cols), :] = value[rows_depth:, :]
            for c in range(2):
                to = pl.multiple_of((c * CORES + half) * part, part)
                newest[pl.ds(to, part), :] = value[c * part : (c + 1) * part, :]
        if shares == 1:
            only = jnp.where(core == 0, keep[rows_depth:, :], swapped[rows_depth:, :])
            for a in range(TGT):
                out[a, depth:, :] = only
        for a in range(TGT):
            out[a, :depth, :] = main[...]

    return call(
        kernel,
        "copies",
        [
            jax.ShapeDtypeStruct((TGT, depth + shares * cols, n), F32),
            jax.ShapeDtypeStruct((CORES * rows_depth, n), F32),
        ],
        [VMEM] * 3,
        main,
        keep,
        swapped,
    )


def per_device(history, self_energy, green_row, propagator):
    _, local_s, local_t, n, _ = history.shape
    half_t = local_t // CORES
    band = n // CHIPS
    sub = band // CORES
    depth = 2 * half_t * band
    rows_depth = 2 * half_t * sub
    in_hbm = lambda value: pltpu.with_memory_space_constraint(value, pltpu.HBM)
    history, self_energy, green_row, propagator = (
        in_hbm(value) for value in (history, self_energy, green_row, propagator)
    )
    scale = MIXING * float(local_s * HIST * n) ** -0.5
    theirs, far_split, near_split, energy, near_rows, prop = collide_first(
        self_energy, history, propagator, green_row, scale
    )
    splits = (near_split, far_split)
    kept, sent, outs = [near_rows.reshape(rows_depth, n)], [], []
    spread = energy
    for step in range(STEPS):
        final_step = step == STEPS - 1

        def sums(far):
            if final_step:
                return collide_last(
                    spread, splits, prop, (kept, sent), step, scale, local_s, half_t, far
                )
            rows = sent if far else kept
            return collide(spread, splits[far], prop, rows, step, scale, local_s, half_t)

        if step:
            theirs = sums(True)
        other = lax.ppermute(theirs, "hist", PARTNER)
        mine = sums(False)
        pieces = join(mine, other, band, half_t, not final_step)
        got = lax.all_to_all(pieces, "hist", 0, 0, axis_index_groups=CHIP_GROUPS)
        got = got.reshape(pieces.shape)
        if final_step:
            break
        main, keep, send = add_up(got, sub, depth)
        moved = lax.ppermute(main, ("tgt", "hist"), TURN)
        swapped = lax.ppermute(send, "hist", PARTNER)
        kept = (kept if step else []) + [keep]
        sent = sent + [swapped]
        spread, newest = copies(moved, keep, swapped, rows_depth, min(step + 1, CORES))
        outs.append(newest)
        spread = lax.all_to_all(
            spread, ("tgt", "hist"), 0, 0, axis_index_groups=TGT_GROUPS
        ).reshape(spread.shape)
    return add_last(got, outs).reshape(STEPS, 2, local_t, sub, n)


def solution(mesh):
    in_specs = (
        P(None, "hist", "tgt", None, None),
        P(None, "hist", None, None),
        P(None, "tgt", None, None),
        P(),
    )
    out_specs = P(None, None, "tgt", "hist", None)
    return jax.shard_map(
        per_device, mesh=mesh, in_specs=in_specs, out_specs=out_specs, check_vma=False
    )
```

```python
import jax
import jax.numpy as jnp
import numpy as np
from jax import lax
from jax.experimental import pallas as pl
from jax.experimental.pallas import tpu as pltpu
from jax.sharding import PartitionSpec as P

STEPS = 4
COUPLING = 1.5
MIXING = 0.7
CHIPS = 8
CORES = 2
TGT = 8
HIST = CHIPS * CORES

ROUTE = np.array(
    [
        (4, 6, 0, 2, 5, 7, 1, 3),
        (5, 4, 7, 3, 1, 6, 2, 0),
        (2, 0, 6, 4, 3, 1, 7, 5),
        (1, 5, 7, 6, 3, 2, 0, 4),
        (3, 7, 5, 4, 1, 0, 2, 6),
        (2, 0, 6, 4, 3, 1, 7, 5),
        (7, 5, 1, 6, 4, 0, 3, 2),
        (4, 6, 0, 2, 5, 7, 1, 3),
    ],
    np.int32,
)
CHIP_ORDER = ((0, 5, 2, 7, 4, 1, 6, 3), (3, 6, 1, 4, 7, 2, 5, 0))
TGT_ORDER = ((0, 1, 3, 2, 4, 5, 7, 6), (0, 1, 3, 2, 4, 5, 7, 6))
CHIP_GROUPS = [[CORES * w + c for w in CHIP_ORDER[c]] for c in range(CORES)]
TGT_GROUPS = [
    [a * HIST + CORES * w + c for a in TGT_ORDER[c]] for w in range(CHIPS) for c in range(CORES)
]
ROUTE_BITS = [
    [sum(TGT_ORDER[c].index(int(ROUTE[x, w])) << (3 * x) for x in range(CHIPS)) for c in range(CORES)]
    for w in range(CHIPS)
]
PARTNER = [(h, h ^ 1) for h in range(HIST)]
TURN = [
    (a * HIST + h, int(ROUTE[a][h // CORES]) * HIST + CORES * a + h % CORES)
    for a in range(TGT)
    for h in range(HIST)
]


VMEM = pl.BlockSpec(memory_space=pltpu.VMEM)
HBM = pl.BlockSpec(memory_space=pltpu.HBM)
F32 = jnp.float32
BF16 = jnp.bfloat16


def call(kernel, name, outs, specs, *args, scratch=(), limit=16):
    return pl.pallas_call(
        kernel,
        out_shape=outs,
        in_specs=specs,
        out_specs=[VMEM] * len(outs),
        scratch_shapes=scratch,
        compiler_params=pltpu.CompilerParams(vmem_limit_bytes=limit * 2**20),
        name=name,
    )(*args)


def seat():
    index = lax.axis_index("hist").astype(jnp.int32)
    return index, index & (CORES - 1)


def of_core(core, choices):
    even, odd = choices
    return even if even == odd else jnp.where(core == 0, jnp.int32(even), jnp.int32(odd))


def route(index, core):
    shift = 3 * (index >> 1)
    return [(jnp.int32(of_core(core, bits)) >> shift) & (TGT - 1) for bits in ROUTE_BITS]


def saturated(real, imag):
    modulus = real * real + imag * imag
    factor = -COUPLING * modulus / (1.0 + modulus)
    return factor * real, factor * imag


def halves(value):
    high = value.astype(BF16)
    return high, (value - high.astype(F32)).astype(BF16)


def dot(left, right, at=1):
    return lax.dot_general(left, right, (((at,), (0,)), ((), ())), preferred_element_type=F32)


def wide(real, imag):
    return jnp.concatenate(
        [jnp.concatenate([real, -imag], 1), jnp.concatenate([imag, real], 1)], 0
    )


def side_terms(prop, cols, rows, slots, scale, half_t):
    sub = prop.shape[1]
    lefts = [(prop[0], prop[1])]
    for m in range(slots):
        real, imag = saturated(*cols(m))
        lefts.append((scale * imag, -scale * real))
    left = []
    for real, imag in lefts:
        left += [jnp.concatenate([real, imag], 1), jnp.concatenate([-imag, real], 1)]
    right = []
    for value in [rows[-1]] + list(rows[:slots]):
        for c in range(2):
            right.append(
                jnp.concatenate(
                    [value[(c * half_t + t) * sub : (c * half_t + t + 1) * sub] for t in range(half_t)], 1
                )
            )
    left_high, left_low = halves(jnp.concatenate(left, 0))
    right_high, right_low = halves(jnp.concatenate(right, 0))
    return dot(left_high, right_high, 0) + (dot(left_high, right_low, 0) + dot(left_low, right_high, 0))


def store_pieces(whole, out, half_t, n, band):
    for w in range(CHIPS):
        for c in range(2):
            for t in range(half_t):
                at = (c * half_t + t) * band
                out[w, at : at + band, :] = whole[
                    c * n + w * band : c * n + (w + 1) * band, t * n : (t + 1) * n
                ]


def collide_first(energy, history, propagator, green, scale):
    _, local_s, local_t, n, _ = history.shape
    half_t = local_t // CORES
    band = n // CHIPS
    sub = band // CORES

    def kernel(
        energy, history, prop, green,
        out, far_split, near_fetched, lefts, near_rows, prop_band,
        far_fetched, far_rows, whole, turned, arrived,
    ):
        index, core = seat()
        at = pl.multiple_of(index * sub, sub)
        count = iter(range(3 * local_s + 3))
        move = lambda source, target: pltpu.make_async_copy(source, target, arrived.at[next(count)])
        span = lambda half: pl.ds(half * half_t, half_t)
        far, near, left_moves = [], [], []
        for s in range(local_s):
            left_moves.append(move(energy.at[:, s], lefts.at[s]))
            far.append(move(history.at[:, s, span(1 - core)], far_fetched.at[s]))
        side = [
            move(green.at[:, span(1 - core), pl.ds(at, sub)], far_rows),
            move(prop, whole),
        ]
        for s in range(local_s):
            near.append(move(history.at[:, s, span(core)], near_fetched.at[s]))
        late = move(green.at[:, span(core), pl.ds(at, sub)], near_rows)
        for pair in zip(left_moves, far):
            for copy in pair:
                copy.start()
        for copy in side + near + [late]:
            copy.start()

        def block(fetched, s):
            return halves(
                jnp.concatenate(
                    [jnp.concatenate([fetched[s, c, t] for t in range(half_t)], 1) for c in range(2)], 0
                )
            )

        total = jnp.zeros((2 * n, half_t * n), F32)
        for s in range(local_s):
            left_moves[s].wait()
            left_high, left_low = halves(wide(scale * lefts[s, 1], -scale * lefts[s, 0]))
            far[s].wait()
            right_high, right_low = block(far_fetched, s)
            rows_at = slice(2 * n * s, 2 * n * (s + 1))
            far_split[0, rows_at, :] = right_high
            far_split[1, rows_at, :] = right_low
            total = total + dot(left_high, right_high)
            total = total + dot(left_high, right_low)
            total = total + dot(left_low, right_high)
        for copy in side:
            copy.wait()
        for c in range(2):
            turned[...] = MIXING * whole[c].T
            prop_band[c] = turned[pl.ds(at, sub), :]
        total = total + side_terms(
            prop_band, None, [far_rows[...].reshape(2 * half_t * sub, n)], 0, scale, half_t
        )
        store_pieces(total, out, half_t, n, band)
        for s in range(local_s):
            near[s].wait()
        late.wait()

    split = jax.ShapeDtypeStruct((2, 2 * n * local_s, half_t * n), BF16)
    fetched = pltpu.VMEM((local_s, 2, half_t, n, n), F32)
    return call(
        kernel,
        "collide_first",
        [
            jax.ShapeDtypeStruct((CHIPS, 2 * half_t * band, n), F32),
            split,
            jax.ShapeDtypeStruct((local_s, 2, half_t, n, n), F32),
            jax.ShapeDtypeStruct((local_s, 2, n, n), F32),
            jax.ShapeDtypeStruct((2, half_t, sub, n), F32),
            jax.ShapeDtypeStruct((2, sub, n), F32),
        ],
        [HBM] * 4,
        energy,
        history,
        propagator,
        green,
        scratch=[
            fetched,
            pltpu.VMEM((2, half_t, sub, n), F32),
            pltpu.VMEM((2, n, n), F32),
            pltpu.VMEM((n, n), F32),
            pltpu.SemaphoreType.DMA((3 * local_s + 3,)),
        ],
    )


def collide_near(energy, fetched, prop, rows, scale):
    local_s, _, half_t, n, _ = fetched.shape
    band = n // CHIPS

    def kernel(energy, fetched, prop, rows, out, split):
        total = side_terms(prop, None, [rows[...]], 0, scale, half_t)
        for s in range(local_s):
            left_high, left_low = halves(wide(scale * energy[s, 1], -scale * energy[s, 0]))
            right_high, right_low = halves(
                jnp.concatenate(
                    [jnp.concatenate([fetched[s, c, t] for t in range(half_t)], 1) for c in range(2)], 0
                )
            )
            at = slice(2 * n * s, 2 * n * (s + 1))
            split[0, at, :] = right_high
            split[1, at, :] = right_low
            total = total + dot(left_high, right_high)
            total = total + dot(left_high, right_low)
            total = total + dot(left_low, right_high)
        store_pieces(total, out, half_t, n, band)

    return call(
        kernel,
        "collide_near",
        [
            jax.ShapeDtypeStruct((CHIPS, 2 * half_t * band, n), F32),
            jax.ShapeDtypeStruct((2, 2 * n * local_s, half_t * n), BF16),
        ],
        [VMEM] * 4,
        energy,
        fetched,
        prop,
        rows,
    )


def slot_cols(spread, core, m, half_t, band, sub):
    a = of_core(core, [order.index(m // 2) for order in TGT_ORDER])
    at = 2 * half_t * band + (m % 2) * 2 * sub
    return spread[a, at : at + sub, :], spread[a, at + sub : at + 2 * sub, :]


def collide(spread, split, prop, rows, slots, scale, local_s, half_t):
    n = spread.shape[-1]
    band = n // CHIPS
    sub = band // CORES

    def kernel(spread, split, prop, *refs):
        rows, out = [ref[...] for ref in refs[:-1]], refs[-1]
        index, core = seat()
        order = route(index, core)
        highs, lows = [], []
        for s in range(local_s):
            if slots == 0:
                real, imag = spread[s, 0], spread[s, 1]
            else:
                real, imag = saturated(
                    *(
                        jnp.concatenate(
                            [
                                spread[
                                    order[w], (c * half_t + s) * band : (c * half_t + s + 1) * band, :
                                ]
                                for w in range(CHIPS)
                            ],
                            0,
                        )
                        for c in range(2)
                    )
                )
            gain = scale if s or not slots else jnp.where(index < slots, 0.0, scale)
            high, low = halves(wide(gain * imag, -gain * real))
            highs.append(high)
            lows.append(low)
        high, low = jnp.concatenate(highs, 1), jnp.concatenate(lows, 1)
        cols = lambda m: slot_cols(spread, core, m, half_t, band, sub)
        total = side_terms(prop, cols, rows, slots, scale, half_t)
        both = dot(jnp.concatenate([high, low], 0), split[0])
        total = total + dot(high, split[1])
        total = total + (both[: 2 * n] + both[2 * n :])
        store_pieces(total, out, half_t, n, band)

    return call(
        kernel,
        "collide",
        [jax.ShapeDtypeStruct((CHIPS, 2 * half_t * band, n), F32)],
        [VMEM] * (3 + len(rows)),
        spread,
        split,
        prop,
        *rows,
    )[0]


def collide_last(spread, splits, prop, rows, slots, scale, local_s, half_t, far):
    n = spread.shape[-1]
    band = n // CHIPS
    sub = band // CORES
    local_t = CORES * half_t

    def kernel(spread, near_split, far_split, prop, *refs):
        near_rows, far_rows = refs[:slots], refs[slots : 2 * slots]
        out, side = refs[2 * slots :]
        index, near = seat()
        order = route(index, near)
        pick = 1 - near if far else near
        cols = lambda m: slot_cols(spread, near, m, half_t, band, sub)
        highs, lows = [], []
        for s in range(local_s):
            real, imag = saturated(
                *(
                    jnp.concatenate(
                        [
                            spread[
                                order[w],
                                pl.ds(pl.multiple_of((c * half_t + s) * band + pick * sub, sub), sub),
                                :,
                            ]
                            for w in range(CHIPS)
                        ],
                        0,
                    )
                    for c in range(2)
                )
            )
            gain = scale if s else jnp.where(index < slots, 0.0, scale)
            high, low = halves(wide(gain * imag, -gain * real))
            highs.append(high)
            lows.append(low)
        high, low = jnp.concatenate(highs, 1), jnp.concatenate(lows, 1)
        both = jnp.concatenate([high, low], 0)
        for half, split, rows in ((near, near_split, near_rows), (1 - near, far_split, far_rows)):
            side[...] = side_terms(prop, cols, [ref[...] for ref in rows], slots, scale, half_t)
            twice = dot(both, split[0])
            total = dot(high, split[1]) + (twice[:n] + twice[n:])
            for w in range(CHIPS):
                for c in range(2):
                    at = pl.multiple_of(c * n + w * band + pick * sub, sub)
                    rest = side[pl.ds(at, sub), :]
                    for t in range(half_t):
                        to = pl.multiple_of((c * local_t + half * half_t + t) * sub, sub)
                        out[w, pl.ds(to, sub), :] = (
                            rest[:, t * n : (t + 1) * n]
                            + total[
                                c * n // 2 + w * sub : c * n // 2 + (w + 1) * sub, t * n : (t + 1) * n
                            ]
                        )

    return call(
        kernel,
        "collide_last",
        [jax.ShapeDtypeStruct((CHIPS, 2 * local_t * sub, n), F32)],
        [VMEM] * (4 + len(rows[0]) + len(rows[1])),
        spread,
        *splits,
        prop,
        *rows[0],
        *rows[1],
        scratch=[pltpu.VMEM((2 * n, half_t * n), F32)],
    )[0]


def join(mine, other, band, half_t, columns):
    chips, depth, n = mine.shape

    def kernel(mine, other, out):
        _, core = seat()
        slots = [of_core(core, [order.index(w) for order in CHIP_ORDER]) for w in range(chips)]
        both = mine[...] + other[...]
        for w in range(chips):
            out[slots[w], :depth, :] = both[w]
        for c in range(2 * columns):
            at = c * half_t * band
            tile = jnp.concatenate([both[w, at : at + band] for w in range(chips)], 0).T
            for w in range(chips):
                out[slots[w], depth + c * band : depth + (c + 1) * band, :] = tile[
                    w * band : (w + 1) * band
                ]

    shape = (chips, depth + 2 * band * columns, n)
    return call(kernel, "join", [jax.ShapeDtypeStruct(shape, F32)], [VMEM, VMEM], mine, other)[0]


def add_up(got, sub, depth):
    _, tall, n = got.shape
    groups = tall // (CORES * sub)

    def kernel(got, main, keep, send, total):
        parts = [got[w] for w in range(CHIPS)]
        while len(parts) > 1:
            parts = [p + q for p, q in zip(parts[::2], parts[1::2])]
        total[...] = parts[0]
        main[...] = parts[0][:depth]
        _, core = seat()
        for g in range(groups):
            at = pl.multiple_of(g * CORES * sub + core * sub, sub)
            keep[g * sub : (g + 1) * sub, :] = total[pl.ds(at, sub), :]
            at = pl.multiple_of(g * CORES * sub + (1 - core) * sub, sub)
            send[g * sub : (g + 1) * sub, :] = total[pl.ds(at, sub), :]

    part = jax.ShapeDtypeStruct((groups * sub, n), F32)
    return call(
        kernel,
        "add_up",
        [jax.ShapeDtypeStruct((depth, n), F32), part, part],
        [VMEM],
        got,
        scratch=[pltpu.VMEM((tall, n), F32)],
    )


def add_last(got, done):
    _, tall, n = got.shape
    steps = len(done) + 1

    def kernel(got, *refs):
        done, (out, total, sent) = refs[:-3], refs[-3:]
        moves = [
            pltpu.make_async_copy(ref, out.at[k], sent.at[k]) for k, ref in enumerate(done + (total,))
        ]
        for move in moves[:-1]:
            move.start()
        parts = [got[w] for w in range(CHIPS)]
        while len(parts) > 1:
            parts = [p + q for p, q in zip(parts[::2], parts[1::2])]
        total[...] = parts[0]
        moves[-1].start()
        for move in moves:
            move.wait()

    return pl.pallas_call(
        kernel,
        out_shape=jax.ShapeDtypeStruct((steps, tall, n), F32),
        in_specs=[VMEM] * steps,
        out_specs=HBM,
        scratch_shapes=[pltpu.VMEM((tall, n), F32), pltpu.SemaphoreType.DMA((steps,))],
        compiler_params=pltpu.CompilerParams(vmem_limit_bytes=16 * 2**20),
        name="add_last",
    )(got, *done)


def copies(main, keep, swapped, rows_depth, shares):
    depth, n = main.shape
    cols = keep.shape[0] - rows_depth
    part = rows_depth // 2

    def kernel(main, keep, swapped, out, newest):
        _, core = seat()
        for half, value in ((core, keep), (1 - core, swapped)):
            if shares == CORES:
                to = pl.multiple_of(depth + half * cols, cols)
                for a in range(TGT):
                    out[a, pl.ds(to, cols), :] = value[rows_depth:, :]
            for c in range(2):
                to = pl.multiple_of((c * CORES + half) * part, part)
                newest[pl.ds(to, part), :] = value[c * part : (c + 1) * part, :]
        if shares == 1:
            only = jnp.where(core == 0, keep[rows_depth:, :], swapped[rows_depth:, :])
            for a in range(TGT):
                out[a, depth:, :] = only
        for a in range(TGT):
            out[a, :depth, :] = main[...]

    return call(
        kernel,
        "copies",
        [
            jax.ShapeDtypeStruct((TGT, depth + shares * cols, n), F32),
            jax.ShapeDtypeStruct((CORES * rows_depth, n), F32),
        ],
        [VMEM] * 3,
        main,
        keep,
        swapped,
    )


def per_device(history, self_energy, green_row, propagator):
    _, local_s, local_t, n, _ = history.shape
    half_t = local_t // CORES
    band = n // CHIPS
    sub = band // CORES
    depth = 2 * half_t * band
    rows_depth = 2 * half_t * sub
    in_hbm = lambda value: pltpu.with_memory_space_constraint(value, pltpu.HBM)
    history, self_energy, green_row, propagator = (
        in_hbm(value) for value in (history, self_energy, green_row, propagator)
    )
    scale = MIXING * float(local_s * HIST * n) ** -0.5
    theirs, far_split, fetched, energy, near_rows, prop = collide_first(
        self_energy, history, propagator, green_row, scale
    )
    kept, sent, outs = [near_rows.reshape(rows_depth, n)], [], []
    spread = energy
    for step in range(STEPS):
        final_step = step == STEPS - 1

        def sums(far):
            if final_step:
                return collide_last(
                    spread, splits, prop, (kept, sent), step, scale, local_s, half_t, far
                )
            rows = sent if far else kept
            return collide(spread, splits[far], prop, rows, step, scale, local_s, half_t)

        if step:
            theirs = sums(True)
        other = lax.ppermute(theirs, "hist", PARTNER)
        if step:
            mine = sums(False)
        else:
            mine, near_split = collide_near(energy, fetched, prop, kept[0], scale)
            splits = (near_split, far_split)
        pieces = join(mine, other, band, half_t, not final_step)
        got = lax.all_to_all(pieces, "hist", 0, 0, axis_index_groups=CHIP_GROUPS)
        got = got.reshape(pieces.shape)
        if final_step:
            break
        main, keep, send = add_up(got, sub, depth)
        moved = lax.ppermute(main, ("tgt", "hist"), TURN)
        swapped = lax.ppermute(send, "hist", PARTNER)
        kept = (kept if step else []) + [keep]
        sent = sent + [swapped]
        spread, newest = copies(moved, keep, swapped, rows_depth, min(step + 1, CORES))
        outs.append(newest)
        spread = lax.all_to_all(
            spread, ("tgt", "hist"), 0, 0, axis_index_groups=TGT_GROUPS
        ).reshape(spread.shape)
    return add_last(got, outs).reshape(STEPS, 2, local_t, sub, n)


def solution(mesh):
    in_specs = (
        P(None, "hist", "tgt", None, None),
        P(None, "hist", None, None),
        P(None, "tgt", None, None),
        P(),
    )
    out_specs = P(None, None, "tgt", "hist", None)
    return jax.shard_map(
        per_device, mesh=mesh, in_specs=in_specs, out_specs=out_specs, check_vma=False
    )
```
